32 devices in a mesh: clips: 2 (over y), tm: 4 (over z), space: 4 (over x, core).
Axes of the slice: x: 2, y: 2, z: 4, core: 2. Of those that a mesh axis runs over, the one named last changes fastest.
Arguments:
- latent: bfloat16 [16, 8, 16, 16], P(('clips', 'tm'), 'space'), parts along dimension 0, may hold values from -6 to 6
- w_in: bfloat16 [3, 3, 3, 16, 384], replicated, may hold values from -0.3125 to 0.3125
- b_in: float32 [384], replicated, may hold values from -1.5 to 1.5
- gain_in: float32 [384], replicated, may hold values from 0.1 to 1.9
- w_time: bfloat16 [3, 384, 768], replicated, may hold values from -0.1875 to 0.1875
- b_time: float32 [768], replicated, may hold values from -1.5 to 1.5
- w_up: bfloat16 [3, 3, 384, 192], replicated, may hold values from -0.109375 to 0.109375
- b_up: float32 [192], replicated, may hold values from -1.5 to 1.5
Outputs:
- decoded: bfloat16 [32, 16, 32, 192], P(('clips', 'tm'), 'space'), parts along dimension 0
The draws below stay inside these ranges and needn't reach their ends.
There are 2 independent parts, one for each index of `clips`. The reference program is written for one: setup_inputs(seed, part) draws one part's arguments, and reference() takes and returns one part's arrays. A program takes and returns all parts, laid end to end along the dimension named above; an argument that names none is the same for every part. Nothing has to cross between parts.
All inputs are finite; a program needn't handle non-finite values.
Results may differ from the reference program's by a relative error of at most 0.0055.
Values may be sent and summed in bfloat16 or wider, within the bound.
A program may use at most 64 MiB of HBM per device.

```python
import jax
import jax.numpy as jnp
from jax import lax

ZC = 16
CH = 384
CO = 192
W = 16
FRAMES = 8
ROWS = 8


def levels(rng, extent, shards, low, high):
    gain, own = 1.0, jax.random.fold_in(rng, 6)
    for position, parts in shards:
        steps = jnp.exp(jax.random.uniform(jax.random.fold_in(own, position), (parts,), jnp.float32, low / len(shards), high / len(shards)))
        gain = gain * jnp.repeat(steps, extent[position] // parts).reshape([-1 if axis == position else 1 for axis in range(len(extent))])
    return gain


def bell_draw(own_key, shape, spread, limit, cuts=(), kind=jnp.bfloat16):
    loudness = levels(own_key, shape, cuts, -0.22, 0.18) if cuts else 1.0
    entries = jax.random.normal(own_key, shape, jnp.float32) * spread * loudness
    return jnp.minimum(jnp.maximum(entries, -limit), limit).astype(kind)


def setup_inputs(seed: int = 0, part: int = 0) -> dict:
    seeds = jax.random.split(jax.random.key(seed), 9)
    part_splits = jax.random.split(jax.random.fold_in(seeds[8], part), 9)
    return {
        "latent": bell_draw(part_splits[0], (FRAMES, ROWS, W, ZC), 1.0, 6.0, ((0, 4), (1, 4))),
        "w_in": bell_draw(seeds[1], (3, 3, 3, ZC, CH), (27 * ZC) ** -0.5, 0.3125),
        "b_in": bell_draw(seeds[2], (CH,), 0.3, 1.5, (), jnp.float32),
        "gain_in": jnp.clip(1.0 + 0.18 * jax.random.normal(seeds[3], (CH,), jnp.float32), 0.1, 1.9),
        "w_time": bell_draw(seeds[4], (3, CH, 2 * CH), (3 * CH) ** -0.5, 0.1875),
        "b_time": bell_draw(seeds[5], (2 * CH,), 0.3, 1.5, (), jnp.float32),
        "w_up": bell_draw(seeds[6], (3, 3, CH, CO), (9 * CH) ** -0.5, 0.109375),
        "b_up": bell_draw(seeds[7], (CO,), 0.3, 1.5, (), jnp.float32),
    }


EPSILON = 1e-06

def normalize_silu(hidden, gain_in):
    inverse = lax.rsqrt(lax.optimization_barrier(jnp.mean(hidden * hidden, axis=1, keepdims=True)) + EPSILON)
    return jax.nn.silu(hidden * inverse * gain_in).astype(jnp.bfloat16)

def plane_conv(padded_frame, w_up, b_up):
    row_count = padded_frame.shape[0] - 2
    col_count = padded_frame.shape[1] - 2
    tap_list = [padded_frame[row_tap:row_tap + row_count, col_tap:col_tap + col_count, :] for row_tap in range(3) for col_tap in range(3)]
    stacked = jnp.concatenate(tap_list, axis=2).reshape(row_count * col_count, -1)
    result = jnp.dot(stacked, w_up.reshape(stacked.shape[1], -1), preferred_element_type=jnp.float32) + b_up
    return result.astype(jnp.bfloat16).reshape(row_count, col_count, -1)

def reference(latent, w_in, b_in, gain_in, w_time, b_time, w_up, b_up):
    frame_count, row_count, col_count, latent_width = latent.shape
    padded = jnp.pad(latent, ((2, 0), (1, 1), (1, 1), (0, 0)))
    tap_list = [padded[frame_tap:frame_tap + frame_count, row_tap:row_tap + row_count, col_tap:col_tap + col_count, :] for frame_tap in range(3) for row_tap in range(3) for col_tap in range(3)]
    stacked = jnp.concatenate(tap_list, axis=3).reshape(frame_count * row_count * col_count, 27 * latent_width)
    hidden = jnp.dot(stacked, w_in.reshape(27 * latent_width, -1), preferred_element_type=jnp.float32) + b_in
    active = normalize_silu(hidden, gain_in).reshape(frame_count, row_count, col_count, -1)
    feature_width = active.shape[3]
    delayed = jnp.pad(active, ((2, 0), (0, 0), (0, 0), (0, 0)))
    tap_list = [delayed[frame_tap:frame_tap + frame_count] for frame_tap in range(3)]
    stacked = jnp.concatenate(tap_list, axis=3).reshape(frame_count * row_count * col_count, 3 * feature_width)
    timed = (jnp.dot(stacked, w_time.reshape(3 * feature_width, -1), preferred_element_type=jnp.float32) + b_time).astype(jnp.bfloat16)
    timed = timed.reshape(frame_count, row_count, col_count, 2, feature_width)
    doubled = jnp.moveaxis(timed, 3, 1).reshape(2 * frame_count, row_count, col_count, feature_width)
    enlarged = jnp.repeat(jnp.repeat(doubled, 2, axis=1), 2, axis=2)
    padded_up = jnp.pad(enlarged, ((0, 0), (1, 1), (1, 1), (0, 0)))

    def one_frame(padded_frame):
        return plane_conv(padded_frame, w_up, b_up)
    return lax.map(one_frame, padded_up)
```

```python
import functools

import jax
import jax.numpy as jnp
from jax import lax
from jax.experimental import pallas as pl
from jax.experimental.pallas import tpu as pltpu
from jax.sharding import PartitionSpec as P

EPSILON = 1e-06
MESH = pl.DeviceIdType.MESH
LANES = 128


def tap_groups(phase):
    return [(-1, (0,)), (0, (1, 2))] if phase == 0 else [(0, (0, 1)), (1, (2,))]


def kernel(
    sizes,
    lat_hbm,
    w_in_hbm,
    b_in_hbm,
    gain_hbm,
    w_time_hbm,
    b_time_hbm,
    w_up_hbm,
    b_up_hbm,
    out_hbm,
    lat_v,
    ext,
    taps,
    w_in_v,
    w_time_v,
    w_up_v,
    w_phase,
    b_in_v,
    gain_v,
    b_time_v,
    b_up_v,
    active,
    summed,
    shifted,
    wide,
    out_v,
    local_sem,
    w_in_sem,
    out_sem,
    send_sem,
    recv_sem,
):
    tm_count, space_count, reach, frames, rows, cols, zc = sizes
    ch = w_time_v.shape[1]
    co = w_up_v.shape[2]
    halo = 1
    own_rows = rows
    out_rows = rows + 2
    tm = lax.axis_index("tm")
    space = lax.axis_index("space")
    offsets = [(d, o) for d in range(reach, -1, -1) for o in (-1, 1, 0) if (d, o) != (0, 0)]

    def inside(d, o):
        t, s = tm + d, space + o
        return (t >= 0) & (t < tm_count) & (s >= 0) & (s < space_count)

    barrier = pltpu.get_barrier_semaphore()
    for d, o in offsets:

        @pl.when(inside(-d, -o))
        def _():
            pl.semaphore_signal(
                barrier, inc=1, device_id={"tm": tm - d, "space": space - o}, device_id_type=MESH
            )

    lat_copy = pltpu.make_async_copy(lat_hbm, lat_v, local_sem.at[0])
    lat_copy.start()
    w_in_copies = [
        pltpu.make_async_copy(w_in_hbm.at[:, b, e], w_in_v.at[:, e, b], w_in_sem.at[3 * b + e])
        for b in range(3)
        for e in range(3)
    ]
    up_copy = pltpu.make_async_copy(w_up_hbm, w_up_v, local_sem.at[1])
    time_copy = pltpu.make_async_copy(w_time_hbm, w_time_v, local_sem.at[2])
    small_copies = [
        pltpu.make_async_copy(src, dst, local_sem.at[3 + i])
        for i, (src, dst) in enumerate(
            ((b_in_hbm, b_in_v), (gain_hbm, gain_v), (b_time_hbm, b_time_v), (b_up_hbm, b_up_v))
        )
    ]
    for copy in [up_copy] + w_in_copies + small_copies + [time_copy]:
        copy.start()

    for d, o in offsets:

        @pl.when(jnp.logical_not(inside(-d, -o)))
        def _():
            ext[reach - d, halo - o] = jnp.zeros(ext.shape[2:], ext.dtype)

    w_in_v[:, :, 3] = jnp.zeros((3, 3) + w_in_v.shape[3:], w_in_v.dtype)

    lat_copy.wait()
    own = lat_v[...].astype(jnp.float32)
    pieces = [own[f, r] for f in range(frames) for r in range(rows)]
    pieces.append(jnp.zeros((cols, LANES - frames * rows * zc), jnp.float32))
    ext[reach, halo] = jnp.concatenate(pieces, axis=1).astype(ext.dtype)

    expected = sum(inside(d, o).astype(jnp.int32) for d, o in offsets)
    pl.semaphore_wait(barrier, expected)

    def remote(d, o):
        slot = (reach - d) * 3 + (halo - o)
        return pltpu.make_async_remote_copy(
            src_ref=ext.at[reach, halo],
            dst_ref=ext.at[reach - d, halo - o],
            send_sem=send_sem.at[slot],
            recv_sem=recv_sem.at[slot],
            device_id={"tm": tm + d, "space": space + o},
            device_id_type=MESH,
        )

    for d, o in offsets:

        @pl.when(inside(d, o))
        def _():
            remote(d, o).start()

    up_copy.wait()
    step = 16

    @pl.loop(0, co // step)
    def _(i):
        at = pl.multiple_of(i * step, step)
        w = [
            [w_up_v[b, e, pl.ds(at, step), :].astype(jnp.float32) for e in range(3)]
            for b in range(3)
        ]
        for q in range(2):
            for m, (_, es) in enumerate(tap_groups(q)):
                col = [sum(w[b][e] for e in es[1:]) + w[b][es[0]] if len(es) > 1 else w[b][es[0]] for b in range(3)]
                for p in range(2):
                    for n, (_, bs) in enumerate(tap_groups(p)):
                        both = col[bs[0]] + col[bs[1]] if len(bs) > 1 else col[bs[0]]
                        place = pl.ds((2 * n + m) * ch, ch)
                        w_phase[p, q, pl.ds(at, step), place] = both.astype(w_phase.dtype)

    for copy in w_in_copies + small_copies:
        copy.wait()

    def arrived(d, o):
        @pl.when(inside(-d, -o))
        def _():
            remote(d, o).wait_recv()

    lane = lax.broadcasted_iota(jnp.int32, (1, LANES), 1)
    col_id = lax.broadcasted_iota(jnp.int32, (out_rows * cols, 1), 0) % cols

    def gather_taps(first, last):
        for frame in range(first, last):
            j, f = divmod(frame, frames)
            base = f * rows * zc
            line = jnp.concatenate(
                [
                    ext[j, k].astype(jnp.float32)[:, base : base + rows * zc]
                    for k in range(3)
                ]
                + [jnp.zeros((cols, LANES - 3 * rows * zc), jnp.float32)],
                axis=1,
            )
            start = rows - 2
            turned = [
                pltpu.roll(line, (LANES - (start + q) * zc) % LANES, 1) if start + q else line
                for q in range(out_rows)
            ]
            mid = jnp.concatenate(turned, axis=0)
            mid = jnp.where(lane < 3 * zc, mid, 0.0)
            left = jnp.where(col_id == 0, 0.0, pltpu.roll(mid, 1, 0))
            right = jnp.where(col_id == cols - 1, 0.0, pltpu.roll(mid, out_rows * cols - 1, 0))
            pair = left + pltpu.roll(mid, 4 * zc, 1)
            taps[frame] = jnp.concatenate([pair, right[:, : 4 * zc]], axis=1).astype(taps.dtype)

    def entry(first, count):
        total = None
        for a in range(3):
            lhs = taps[pl.ds(first + a, count)].reshape(count * out_rows * cols, -1)
            term = jnp.dot(lhs, w_in_v[a].reshape(12 * zc, ch), preferred_element_type=jnp.float32)
            total = term if total is None else total + term
        hidden = total + b_in_v[...].reshape(1, ch)
        inverse = lax.rsqrt(jnp.mean(hidden * hidden, axis=1, keepdims=True) + EPSILON)
        v = hidden * inverse * gain_v[...].reshape(1, ch)
        return (v / (1.0 + jnp.exp(-v))).astype(active.dtype).reshape(count, out_rows * cols, ch)

    head = reach * frames - 4
    for d, o in offsets:
        if d * frames <= frames + 1:
            arrived(d, o)
    gather_taps(head + 2, head + 4 + frames)
    active[pl.ds(2, frames)] = entry(head + 2, frames)
    time_copy.wait()
    size = out_rows * cols

    def times(first, count, tap):
        lhs = active[pl.ds(first, count)].reshape(count * size, ch)
        return jnp.dot(lhs, w_time_v[tap], preferred_element_type=jnp.float32)

    summed[...] = times(2, frames, 2) + b_time_v[...].reshape(1, 2 * ch)
    for tap in range(2):
        skip = 2 - tap
        if frames > skip:
            summed[skip * size :] = summed[skip * size :] + times(2, frames - skip, tap)

    for d, o in offsets:
        if d * frames > frames + 1:
            arrived(d, o)
    gather_taps(head, head + 2)
    early = entry(head, 2)
    known = lax.broadcasted_iota(jnp.int32, (2, 1, 1), 0) + (tm * frames - 2) >= 0
    active[pl.ds(0, 2)] = jnp.where(known, early, jnp.zeros_like(early))
    for tap in range(2):
        n = min(2 - tap, frames)
        summed[: n * size] = summed[: n * size] + times(tap, n, tap)

    row_id = lax.broadcasted_iota(jnp.int32, (frames * size, 1), 0) % size // cols
    column = lax.broadcasted_iota(jnp.int32, (frames * size, 1), 0) % cols
    row_ok = ((row_id > 0) | (space > 0)) & ((row_id < out_rows - 1) | (space < space_count - 1))
    for half in range(2):
        part = summed[:, half * ch : (half + 1) * ch].astype(shifted.dtype).astype(jnp.float32)
        part = jnp.where(row_ok, part, 0.0)
        back = jnp.where(column == 0, 0.0, pltpu.roll(part, 1, 0))
        ahead = jnp.where(column == cols - 1, 0.0, pltpu.roll(part, frames * size - 1, 0))
        for i, moved in enumerate((back, part, ahead)):
            shifted[i, :, half] = moved.astype(shifted.dtype).reshape(frames, out_rows, cols, ch)

    out_copies = []
    for p in range(2):
        for q in range(2):
            lhs = jnp.concatenate(
                [
                    shifted[1 + dc, :, :, pl.ds(1 + dr, own_rows)].reshape(
                        2 * frames * own_rows * cols, ch
                    )
                    for dr, _ in tap_groups(p)
                    for dc, _ in tap_groups(q)
                ],
                axis=1,
            )
            y = lax.dot_general(
                lhs, w_phase[p, q], (((1,), (1,)), ((), ())), preferred_element_type=jnp.float32
            )
            y = y + b_up_v[...].reshape(1, co)
            y = y.reshape(2 * frames, own_rows, cols, co)
            for g in range(2 * frames):
                for r in range(own_rows):
                    part = y[g, r]
                    low = part[:, :LANES]
                    wide[0, g, 2 * r + p, pl.ds(q, cols, stride=2), :] = low
                    rest = jnp.concatenate(
                        [part[:, LANES:], jnp.zeros((cols, 2 * LANES - co), jnp.float32)], axis=1
                    )
                    wide[1, g, 2 * r + p, pl.ds(q, cols, stride=2), :] = rest
        for r in range(own_rows):
            row = 2 * r + p
            out_v[:, row, :, :LANES] = wide[0, :, row].astype(out_v.dtype)
            out_v[:, row, :, LANES:] = wide[1, :, row][:, :, : co - LANES].astype(out_v.dtype)
            copy = pltpu.make_async_copy(out_v.at[:, row], out_hbm.at[:, row], out_sem.at[row])
            copy.start()
            out_copies.append(copy)

    for d, o in offsets:

        @pl.when(inside(d, o))
        def _():
            remote(d, o).wait_send()

    for copy in out_copies:
        copy.wait()


def shards(tm_count, space_count, latent, w_in, b_in, gain_in, w_time, b_time, w_up, b_up):
    frames, rows, cols, zc = latent.shape
    ch, co = w_in.shape[-1], w_up.shape[-1]
    reach = -(-4 // frames)
    out_rows = rows + 2
    size = out_rows * cols
    bf16, f32 = jnp.bfloat16, jnp.float32
    any_spec = pl.BlockSpec(memory_space=pl.ANY)
    return pl.pallas_call(
        functools.partial(kernel, (tm_count, space_count, reach, frames, rows, cols, zc)),
        out_shape=jax.ShapeDtypeStruct((2 * frames, 2 * rows, 2 * cols, co), bf16),
        in_specs=[any_spec] * 8,
        out_specs=any_spec,
        scratch_shapes=[
            pltpu.VMEM(latent.shape, bf16),
            pltpu.VMEM((reach + 1, 3, cols, LANES), bf16),
            pltpu.VMEM(((reach + 1) * frames, size, 12 * zc), bf16),
            pltpu.VMEM((3, 3, 4, zc, ch), bf16),
            pltpu.VMEM(w_time.shape, bf16),
            pltpu.VMEM((3, 3, co, ch), bf16),
            pltpu.VMEM((2, 2, co, 4 * ch), bf16),
            pltpu.VMEM((ch,), f32),
            pltpu.VMEM((ch,), f32),
            pltpu.VMEM((2 * ch,), f32),
            pltpu.VMEM((co,), f32),
            pltpu.VMEM((frames + 2, size, ch), bf16),
            pltpu.VMEM((frames * size, 2 * ch), f32),
            pltpu.VMEM((3, frames, 2, out_rows, cols, ch), bf16),
            pltpu.VMEM((2, 2 * frames, 2 * rows, 2 * cols, LANES), f32),
            pltpu.VMEM((2 * frames, 2 * rows, 2 * cols, co), bf16),
            pltpu.SemaphoreType.DMA((7,)),
            pltpu.SemaphoreType.DMA((9,)),
            pltpu.SemaphoreType.DMA((2 * rows,)),
            pltpu.SemaphoreType.DMA(((reach + 1) * 3,)),
            pltpu.SemaphoreType.DMA(((reach + 1) * 3,)),
        ],
        compiler_params=pltpu.CompilerParams(collective_id=0, has_side_effects=True),
    )(
        latent,
        w_in,
        b_in,
        gain_in,
        w_time,
        b_time,
        jnp.swapaxes(w_up, 2, 3),
        b_up,
    )


def solution(mesh):
    in_specs = (P(("clips", "tm"), "space", None, None), P(), P(), P(), P(), P(), P(), P())
    out_specs = P(("clips", "tm"), "space", None, None)
    body = functools.partial(shards, mesh.shape["tm"], mesh.shape["space"])
    return jax.shard_map(body, mesh=mesh, in_specs=in_specs, out_specs=out_specs, check_vma=False)
```

```python
import functools

import jax
import jax.numpy as jnp
from jax import lax
from jax.experimental import pallas as pl
from jax.experimental.pallas import tpu as pltpu
from jax.sharding import PartitionSpec as P

EPSILON = 1e-06
MESH = pl.DeviceIdType.MESH
LANES = 128
VMEM_BYTES = 67043328


def tap_groups(phase):
    return [(-1, (0,)), (0, (1, 2))] if phase == 0 else [(0, (0, 1)), (1, (2,))]


def kernel(
    sizes,
    lat_hbm,
    w_in_hbm,
    b_in_hbm,
    gain_hbm,
    w_time_hbm,
    b_time_hbm,
    w_up_hbm,
    b_up_hbm,
    out_v,
    lat_v,
    ext,
    taps,
    w_in_v,
    w_time_v,
    w_up_v,
    w_phase,
    b_in_v,
    gain_v,
    b_time_v,
    b_up_v,
    active,
    summed,
    shifted,
    wide,
    local_sem,
    w_in_sem,
    send_sem,
    recv_sem,
):
    tm_count, space_count, reach, frames, rows, cols, zc = sizes
    ch = w_time_v.shape[1]
    co = w_up_v.shape[2]
    halo = 1
    own_rows = rows
    out_rows = rows + 2
    tm = lax.axis_index("tm")
    space = lax.axis_index("space")
    offsets = [(d, o) for d in range(reach, -1, -1) for o in (-1, 1, 0) if (d, o) != (0, 0)]

    def inside(d, o):
        t, s = tm + d, space + o
        return (t >= 0) & (t < tm_count) & (s >= 0) & (s < space_count)

    barrier = pltpu.get_barrier_semaphore()
    for d, o in offsets:

        @pl.when(inside(-d, -o))
        def _():
            pl.semaphore_signal(
                barrier, inc=1, device_id={"tm": tm - d, "space": space - o}, device_id_type=MESH
            )

    lat_copy = pltpu.make_async_copy(lat_hbm, lat_v, local_sem.at[0])
    lat_copy.start()
    w_in_copies = [
        pltpu.make_async_copy(w_in_hbm.at[:, b, e], w_in_v.at[:, e, b], w_in_sem.at[3 * b + e])
        for b in range(3)
        for e in range(3)
    ]
    up_copy = pltpu.make_async_copy(w_up_hbm, w_up_v, local_sem.at[1])
    time_copy = pltpu.make_async_copy(w_time_hbm, w_time_v, local_sem.at[2])
    small_copies = [
        pltpu.make_async_copy(src, dst, local_sem.at[3 + i])
        for i, (src, dst) in enumerate(
            ((b_in_hbm, b_in_v), (gain_hbm, gain_v), (b_time_hbm, b_time_v), (b_up_hbm, b_up_v))
        )
    ]
    for copy in [up_copy] + w_in_copies + small_copies + [time_copy]:
        copy.start()

    for d, o in offsets:

        @pl.when(jnp.logical_not(inside(-d, -o)))
        def _():
            ext[reach - d, halo - o] = jnp.zeros(ext.shape[2:], ext.dtype)

    w_in_v[:, :, 3] = jnp.zeros((3, 3) + w_in_v.shape[3:], w_in_v.dtype)

    lat_copy.wait()
    own = lat_v[...].astype(jnp.float32)
    pieces = [own[f, r] for f in range(frames) for r in range(rows)]
    pieces.append(jnp.zeros((cols, LANES - frames * rows * zc), jnp.float32))
    ext[reach, halo] = jnp.concatenate(pieces, axis=1).astype(ext.dtype)

    expected = sum(inside(d, o).astype(jnp.int32) for d, o in offsets)
    pl.semaphore_wait(barrier, expected)

    def remote(d, o):
        slot = (reach - d) * 3 + (halo - o)
        return pltpu.make_async_remote_copy(
            src_ref=ext.at[reach, halo],
            dst_ref=ext.at[reach - d, halo - o],
            send_sem=send_sem.at[slot],
            recv_sem=recv_sem.at[slot],
            device_id={"tm": tm + d, "space": space + o},
            device_id_type=MESH,
        )

    for d, o in offsets:

        @pl.when(inside(d, o))
        def _():
            remote(d, o).start()

    up_copy.wait()
    step = 16

    @pl.loop(0, co // step)
    def _(i):
        at = pl.multiple_of(i * step, step)
        w = [
            [w_up_v[b, e, pl.ds(at, step), :].astype(jnp.float32) for e in range(3)]
            for b in range(3)
        ]
        for q in range(2):
            for m, (_, es) in enumerate(tap_groups(q)):
                col = [sum(w[b][e] for e in es[1:]) + w[b][es[0]] if len(es) > 1 else w[b][es[0]] for b in range(3)]
                for p in range(2):
                    for n, (_, bs) in enumerate(tap_groups(p)):
                        both = col[bs[0]] + col[bs[1]] if len(bs) > 1 else col[bs[0]]
                        place = pl.ds((2 * n + m) * ch, ch)
                        w_phase[p, q, pl.ds(at, step), place] = both.astype(w_phase.dtype)

    for copy in w_in_copies + small_copies:
        copy.wait()

    def arrived(d, o):
        @pl.when(inside(-d, -o))
        def _():
            remote(d, o).wait_recv()

    lane = lax.broadcasted_iota(jnp.int32, (1, LANES), 1)
    col_id = lax.broadcasted_iota(jnp.int32, (out_rows * cols, 1), 0) % cols

    def gather_taps(first, last):
        for frame in range(first, last):
            j, f = divmod(frame, frames)
            base = f * rows * zc
            line = jnp.concatenate(
                [
                    ext[j, k].astype(jnp.float32)[:, base : base + rows * zc]
                    for k in range(3)
                ]
                + [jnp.zeros((cols, LANES - 3 * rows * zc), jnp.float32)],
                axis=1,
            )
            start = rows - 2
            turned = [
                pltpu.roll(line, (LANES - (start + q) * zc) % LANES, 1) if start + q else line
                for q in range(out_rows)
            ]
            mid = jnp.concatenate(turned, axis=0)
            mid = jnp.where(lane < 3 * zc, mid, 0.0)
            left = jnp.where(col_id == 0, 0.0, pltpu.roll(mid, 1, 0))
            right = jnp.where(col_id == cols - 1, 0.0, pltpu.roll(mid, out_rows * cols - 1, 0))
            pair = left + pltpu.roll(mid, 4 * zc, 1)
            taps[frame] = jnp.concatenate([pair, right[:, : 4 * zc]], axis=1).astype(taps.dtype)

    def entry(first, count):
        total = None
        for a in range(3):
            lhs = taps[pl.ds(first + a, count)].reshape(count * out_rows * cols, -1)
            term = jnp.dot(lhs, w_in_v[a].reshape(12 * zc, ch), preferred_element_type=jnp.float32)
            total = term if total is None else total + term
        hidden = total + b_in_v[...].reshape(1, ch)
        inverse = lax.rsqrt(jnp.mean(hidden * hidden, axis=1, keepdims=True) + EPSILON)
        v = hidden * inverse * gain_v[...].reshape(1, ch)
        return (v / (1.0 + jnp.exp(-v))).astype(active.dtype).reshape(count, out_rows * cols, ch)

    head = reach * frames - 4
    for d, o in offsets:
        if d * frames <= frames + 1:
            arrived(d, o)
    gather_taps(head + 2, head + 4 + frames)
    active[pl.ds(2, frames)] = entry(head + 2, frames)
    time_copy.wait()
    size = out_rows * cols

    def times(first, count, tap):
        lhs = active[pl.ds(first, count)].reshape(count * size, ch)
        return jnp.dot(lhs, w_time_v[tap], preferred_element_type=jnp.float32)

    summed[...] = times(2, frames, 2) + b_time_v[...].reshape(1, 2 * ch)
    for tap in range(2):
        skip = 2 - tap
        if frames > skip:
            summed[skip * size :] = summed[skip * size :] + times(2, frames - skip, tap)

    for d, o in offsets:
        if d * frames > frames + 1:
            arrived(d, o)
    gather_taps(head, head + 2)
    early = entry(head, 2)
    known = lax.broadcasted_iota(jnp.int32, (2, 1, 1), 0) + (tm * frames - 2) >= 0
    active[pl.ds(0, 2)] = jnp.where(known, early, jnp.zeros_like(early))
    for tap in range(2):
        n = min(2 - tap, frames)
        summed[: n * size] = summed[: n * size] + times(tap, n, tap)

    row_id = lax.broadcasted_iota(jnp.int32, (frames * size, 1), 0) % size // cols
    column = lax.broadcasted_iota(jnp.int32, (frames * size, 1), 0) % cols
    row_ok = ((row_id > 0) | (space > 0)) & ((row_id < out_rows - 1) | (space < space_count - 1))
    for half in range(2):
        part = summed[:, half * ch : (half + 1) * ch].astype(shifted.dtype).astype(jnp.float32)
        part = jnp.where(row_ok, part, 0.0)
        back = jnp.where(column == 0, 0.0, pltpu.roll(part, 1, 0))
        ahead = jnp.where(column == cols - 1, 0.0, pltpu.roll(part, frames * size - 1, 0))
        for i, moved in enumerate((back, part, ahead)):
            shifted[i, :, half] = moved.astype(shifted.dtype).reshape(frames, out_rows, cols, ch)

    for p in range(2):
        for q in range(2):
            lhs = jnp.concatenate(
                [
                    shifted[1 + dc, :, :, pl.ds(1 + dr, own_rows)].reshape(
                        2 * frames * own_rows * cols, ch
                    )
                    for dr, _ in tap_groups(p)
                    for dc, _ in tap_groups(q)
                ],
                axis=1,
            )
            y = lax.dot_general(
                lhs, w_phase[p, q], (((1,), (1,)), ((), ())), preferred_element_type=jnp.float32
            )
            y = y + b_up_v[...].reshape(1, co)
            y = y.reshape(2 * frames, own_rows, cols, co)
            for g in range(2 * frames):
                for r in range(own_rows):
                    part = y[g, r]
                    low = part[:, :LANES]
                    wide[0, g, 2 * r + p, pl.ds(q, cols, stride=2), :] = low
                    rest = jnp.concatenate(
                        [part[:, LANES:], jnp.zeros((cols, 2 * LANES - co), jnp.float32)], axis=1
                    )
                    wide[1, g, 2 * r + p, pl.ds(q, cols, stride=2), :] = rest
        for r in range(own_rows):
            row = 2 * r + p
            out_v[:, row, :, :LANES] = wide[0, :, row].astype(out_v.dtype)
            out_v[:, row, :, LANES:] = wide[1, :, row][:, :, : co - LANES].astype(out_v.dtype)

    for d, o in offsets:

        @pl.when(inside(d, o))
        def _():
            remote(d, o).wait_send()


def shards(tm_count, space_count, latent, w_in, b_in, gain_in, w_time, b_time, w_up, b_up):
    frames, rows, cols, zc = latent.shape
    ch, co = w_in.shape[-1], w_up.shape[-1]
    reach = -(-4 // frames)
    out_rows = rows + 2
    size = out_rows * cols
    bf16, f32 = jnp.bfloat16, jnp.float32
    any_spec = pl.BlockSpec(memory_space=pl.ANY)
    return pl.pallas_call(
        functools.partial(kernel, (tm_count, space_count, reach, frames, rows, cols, zc)),
        out_shape=pltpu.VMEM((2 * frames, 2 * rows, 2 * cols, co), bf16),
        in_specs=[any_spec] * 8,
        out_specs=pl.BlockSpec(memory_space=pltpu.VMEM),
        scratch_shapes=[
            pltpu.VMEM(latent.shape, bf16),
            pltpu.VMEM((reach + 1, 3, cols, LANES), bf16),
            pltpu.VMEM(((reach + 1) * frames, size, 12 * zc), bf16),
            pltpu.VMEM((3, 3, 4, zc, ch), bf16),
            pltpu.VMEM(w_time.shape, bf16),
            pltpu.VMEM((3, 3, co, ch), bf16),
            pltpu.VMEM((2, 2, co, 4 * ch), bf16),
            pltpu.VMEM((ch,), f32),
            pltpu.VMEM((ch,), f32),
            pltpu.VMEM((2 * ch,), f32),
            pltpu.VMEM((co,), f32),
            pltpu.VMEM((frames + 2, size, ch), bf16),
            pltpu.VMEM((frames * size, 2 * ch), f32),
            pltpu.VMEM((3, frames, 2, out_rows, cols, ch), bf16),
            pltpu.VMEM((2, 2 * frames, 2 * rows, 2 * cols, LANES), f32),
            pltpu.SemaphoreType.DMA((7,)),
            pltpu.SemaphoreType.DMA((9,)),
            pltpu.SemaphoreType.DMA(((reach + 1) * 3,)),
            pltpu.SemaphoreType.DMA(((reach + 1) * 3,)),
        ],
        compiler_params=pltpu.CompilerParams(collective_id=0, has_side_effects=True, vmem_limit_bytes=VMEM_BYTES - 2 * frames * 2 * rows * 2 * cols * (-(-co // LANES) * LANES) * 2),
    )(
        latent,
        w_in,
        b_in,
        gain_in,
        w_time,
        b_time,
        jnp.swapaxes(w_up, 2, 3),
        b_up,
    )


def solution(mesh):
    in_specs = (P(("clips", "tm"), "space", None, None), P(), P(), P(), P(), P(), P(), P())
    out_specs = P(("clips", "tm"), "space", None, None)
    body = functools.partial(shards, mesh.shape["tm"], mesh.shape["space"])
    return jax.shard_map(body, mesh=mesh, in_specs=in_specs, out_specs=out_specs, check_vma=False)
```

```python
import functools

import jax
import jax.numpy as jnp
from jax import lax
from jax.experimental import pallas as pl
from jax.experimental.pallas import tpu as pltpu
from jax.sharding import PartitionSpec as P

EPSILON = 1e-06
MESH = pl.DeviceIdType.MESH
LANES = 128
VMEM_BYTES = 67043328


def tap_groups(phase):
    return [(-1, (0,)), (0, (1, 2))] if phase == 0 else [(0, (0, 1)), (1, (2,))]


def kernel(
    sizes,
    lat_hbm,
    w_in_hbm,
    b_in_hbm,
    gain_hbm,
    w_time_hbm,
    b_time_hbm,
    w_up_hbm,
    b_up_hbm,
    out_v,
    lat_v,
    ext,
    taps,
    w_in_v,
    w_time_v,
    w_up_v,
    w_phase,
    b_in_v,
    gain_v,
    b_time_v,
    b_up_v,
    active,
    summed,
    shifted,
    wide,
    local_sem,
    w_in_sem,
    send_sem,
    recv_sem,
):
    tm_count, space_count, reach, frames, rows, cols, zc = sizes
    ch = w_time_v.shape[1]
    co = w_up_v.shape[2]
    halo = 1
    own_rows = rows
    out_rows = rows + 2
    tm = lax.axis_index("tm")
    space = lax.axis_index("space")
    low, high = space > 0, space < space_count - 1
    later = tm < tm_count - 1

    barrier = pltpu.get_barrier_semaphore()
    for there, target in (
        (low, {"space": space - 1}),
        (high, {"space": space + 1}),
        (tm > 0, {"tm": tm - 1}),
    ):

        @pl.when(there)
        def _():
            pl.semaphore_signal(barrier, inc=1, device_id=target, device_id_type=MESH)

    lat_copy = pltpu.make_async_copy(lat_hbm, lat_v, local_sem.at[0])
    lat_copy.start()
    w_in_copies = [
        pltpu.make_async_copy(w_in_hbm.at[:, b, e], w_in_v.at[:, e, b], w_in_sem.at[3 * b + e])
        for b in range(3)
        for e in range(3)
    ]
    up_copy = pltpu.make_async_copy(w_up_hbm, w_up_v, local_sem.at[1])
    time_copy = pltpu.make_async_copy(w_time_hbm, w_time_v, local_sem.at[2])
    small_copies = [
        pltpu.make_async_copy(src, dst, local_sem.at[3 + i])
        for i, (src, dst) in enumerate(
            ((b_in_hbm, b_in_v), (gain_hbm, gain_v), (b_time_hbm, b_time_v), (b_up_hbm, b_up_v))
        )
    ]
    for copy in [up_copy] + w_in_copies + small_copies + [time_copy]:
        copy.start()

    for there, k in ((low, 0), (high, 2)):

        @pl.when(jnp.logical_not(there))
        def _():
            ext[reach, k] = jnp.zeros(ext.shape[2:], ext.dtype)

    for h in range(1, reach + 1):

        @pl.when(tm < h)
        def _():
            ext[reach - h] = jnp.zeros(ext.shape[1:], ext.dtype)

    w_in_v[:, :, 3] = jnp.zeros((3, 3) + w_in_v.shape[3:], w_in_v.dtype)

    lat_copy.wait()
    own = lat_v[...].astype(jnp.float32)
    pieces = [own[f, r] for f in range(frames) for r in range(rows)]
    pieces.append(jnp.zeros((cols, LANES - frames * rows * zc), jnp.float32))
    ext[reach, halo] = jnp.concatenate(pieces, axis=1).astype(ext.dtype)

    pl.semaphore_wait(
        barrier, low.astype(jnp.int32) + high.astype(jnp.int32) + later.astype(jnp.int32)
    )

    def along_rows(o):
        return pltpu.make_async_remote_copy(
            src_ref=ext.at[reach, halo],
            dst_ref=ext.at[reach, halo - o],
            send_sem=send_sem.at[reach + (o + 1) // 2],
            recv_sem=recv_sem.at[reach + (o + 1) // 2],
            device_id={"space": space + o},
            device_id_type=MESH,
        )

    def along_time(h):
        return pltpu.make_async_remote_copy(
            src_ref=ext.at[reach - h + 1],
            dst_ref=ext.at[reach - h],
            send_sem=send_sem.at[h - 1],
            recv_sem=recv_sem.at[h - 1],
            device_id={"tm": tm + 1},
            device_id_type=MESH,
        )

    for there, o in ((low, -1), (high, 1)):

        @pl.when(there)
        def _():
            along_rows(o).start()

    up_copy.wait()
    step = 16

    @pl.loop(0, co // step)
    def _(i):
        at = pl.multiple_of(i * step, step)
        w = [
            [w_up_v[b, e, pl.ds(at, step), :].astype(jnp.float32) for e in range(3)]
            for b in range(3)
        ]
        for q in range(2):
            for m, (_, es) in enumerate(tap_groups(q)):
                col = [sum(w[b][e] for e in es[1:]) + w[b][es[0]] if len(es) > 1 else w[b][es[0]] for b in range(3)]
                for p in range(2):
                    for n, (_, bs) in enumerate(tap_groups(p)):
                        both = col[bs[0]] + col[bs[1]] if len(bs) > 1 else col[bs[0]]
                        place = pl.ds((2 * n + m) * ch, ch)
                        w_phase[p, q, pl.ds(at, step), place] = both.astype(w_phase.dtype)

    for there, o in ((low, 1), (high, -1)):

        @pl.when(there)
        def _():
            along_rows(o).wait_recv()

    def pass_on(h):
        @pl.when(later & (tm >= h - 1))
        def _():
            along_time(h).start()

    def arrived(h):
        @pl.when(tm >= h)
        def _():
            along_time(h).wait_recv()

    pass_on(1)
    for copy in w_in_copies + small_copies:
        copy.wait()

    lane = lax.broadcasted_iota(jnp.int32, (1, LANES), 1)
    col_id = lax.broadcasted_iota(jnp.int32, (out_rows * cols, 1), 0) % cols

    def gather_taps(first, last):
        for frame in range(first, last):
            j, f = divmod(frame, frames)
            base = f * rows * zc
            line = jnp.concatenate(
                [
                    ext[j, k].astype(jnp.float32)[:, base : base + rows * zc]
                    for k in range(3)
                ]
                + [jnp.zeros((cols, LANES - 3 * rows * zc), jnp.float32)],
                axis=1,
            )
            start = rows - 2
            turned = [
                pltpu.roll(line, (LANES - (start + q) * zc) % LANES, 1) if start + q else line
                for q in range(out_rows)
            ]
            mid = jnp.concatenate(turned, axis=0)
            mid = jnp.where(lane < 3 * zc, mid, 0.0)
            left = jnp.where(col_id == 0, 0.0, pltpu.roll(mid, 1, 0))
            right = jnp.where(col_id == cols - 1, 0.0, pltpu.roll(mid, out_rows * cols - 1, 0))
            pair = left + pltpu.roll(mid, 4 * zc, 1)
            taps[frame] = jnp.concatenate([pair, right[:, : 4 * zc]], axis=1).astype(taps.dtype)

    def entry(first, count):
        total = None
        for a in range(3):
            lhs = taps[pl.ds(first + a, count)].reshape(count * out_rows * cols, -1)
            term = jnp.dot(lhs, w_in_v[a].reshape(12 * zc, ch), preferred_element_type=jnp.float32)
            total = term if total is None else total + term
        hidden = total + b_in_v[...].reshape(1, ch)
        inverse = lax.rsqrt(jnp.mean(hidden * hidden, axis=1, keepdims=True) + EPSILON)
        v = hidden * inverse * gain_v[...].reshape(1, ch)
        return (v / (1.0 + jnp.exp(-v))).astype(active.dtype).reshape(count, out_rows * cols, ch)

    head = reach * frames - 4
    near = -(-2 // frames)
    for h in range(1, near + 1):
        arrived(h)
        if h < reach:
            pass_on(h + 1)
    gather_taps(head + 2, head + 4 + frames)
    active[pl.ds(2, frames)] = entry(head + 2, frames)
    time_copy.wait()
    size = out_rows * cols

    def times(first, count, tap):
        lhs = active[pl.ds(first, count)].reshape(count * size, ch)
        return jnp.dot(lhs, w_time_v[tap], preferred_element_type=jnp.float32)

    summed[...] = times(2, frames, 2) + b_time_v[...].reshape(1, 2 * ch)
    for tap in range(2):
        skip = 2 - tap
        if frames > skip:
            summed[skip * size :] = summed[skip * size :] + times(2, frames - skip, tap)

    for h in range(near + 1, reach + 1):
        arrived(h)
        if h < reach:
            pass_on(h + 1)
    gather_taps(head, head + 2)
    early = entry(head, 2)
    known = lax.broadcasted_iota(jnp.int32, (2, 1, 1), 0) + (tm * frames - 2) >= 0
    active[pl.ds(0, 2)] = jnp.where(known, early, jnp.zeros_like(early))
    for tap in range(2):
        n = min(2 - tap, frames)
        summed[: n * size] = summed[: n * size] + times(tap, n, tap)

    row_id = lax.broadcasted_iota(jnp.int32, (frames * size, 1), 0) % size // cols
    column = lax.broadcasted_iota(jnp.int32, (frames * size, 1), 0) % cols
    row_ok = ((row_id > 0) | (space > 0)) & ((row_id < out_rows - 1) | (space < space_count - 1))
    for half in range(2):
        part = summed[:, half * ch : (half + 1) * ch].astype(shifted.dtype).astype(jnp.float32)
        part = jnp.where(row_ok, part, 0.0)
        back = jnp.where(column == 0, 0.0, pltpu.roll(part, 1, 0))
        ahead = jnp.where(column == cols - 1, 0.0, pltpu.roll(part, frames * size - 1, 0))
        for i, moved in enumerate((back, part, ahead)):
            shifted[i, :, half] = moved.astype(shifted.dtype).reshape(frames, out_rows, cols, ch)

    for p in range(2):
        for q in range(2):
            lhs = jnp.concatenate(
                [
                    shifted[1 + dc, :, :, pl.ds(1 + dr, own_rows)].reshape(
                        2 * frames * own_rows * cols, ch
                    )
                    for dr, _ in tap_groups(p)
                    for dc, _ in tap_groups(q)
                ],
                axis=1,
            )
            y = lax.dot_general(
                lhs, w_phase[p, q], (((1,), (1,)), ((), ())), preferred_element_type=jnp.float32
            )
            y = y + b_up_v[...].reshape(1, co)
            y = y.reshape(2 * frames, own_rows, cols, co)
            for g in range(2 * frames):
                for r in range(own_rows):
                    part = y[g, r]
                    first = part[:, :LANES]
                    wide[0, g, 2 * r + p, pl.ds(q, cols, stride=2), :] = first
                    rest = jnp.concatenate(
                        [part[:, LANES:], jnp.zeros((cols, 2 * LANES - co), jnp.float32)], axis=1
                    )
                    wide[1, g, 2 * r + p, pl.ds(q, cols, stride=2), :] = rest
        for r in range(own_rows):
            row = 2 * r + p
            out_v[:, row, :, :LANES] = wide[0, :, row].astype(out_v.dtype)
            out_v[:, row, :, LANES:] = wide[1, :, row][:, :, : co - LANES].astype(out_v.dtype)

    for there, o in ((low, -1), (high, 1)):

        @pl.when(there)
        def _():
            along_rows(o).wait_send()

    for h in range(1, reach + 1):

        @pl.when(later & (tm >= h - 1))
        def _():
            along_time(h).wait_send()


def shards(tm_count, space_count, latent, w_in, b_in, gain_in, w_time, b_time, w_up, b_up):
    frames, rows, cols, zc = latent.shape
    ch, co = w_in.shape[-1], w_up.shape[-1]
    reach = -(-4 // frames)
    out_rows = rows + 2
    size = out_rows * cols
    bf16, f32 = jnp.bfloat16, jnp.float32
    any_spec = pl.BlockSpec(memory_space=pl.ANY)
    return pl.pallas_call(
        functools.partial(kernel, (tm_count, space_count, reach, frames, rows, cols, zc)),
        out_shape=pltpu.VMEM((2 * frames, 2 * rows, 2 * cols, co), bf16),
        in_specs=[any_spec] * 8,
        out_specs=pl.BlockSpec(memory_space=pltpu.VMEM),
        scratch_shapes=[
            pltpu.VMEM(latent.shape, bf16),
            pltpu.VMEM((reach + 1, 3, cols, LANES), bf16),
            pltpu.VMEM(((reach + 1) * frames, size, 12 * zc), bf16),
            pltpu.VMEM((3, 3, 4, zc, ch), bf16),
            pltpu.VMEM(w_time.shape, bf16),
            pltpu.VMEM((3, 3, co, ch), bf16),
            pltpu.VMEM((2, 2, co, 4 * ch), bf16),
            pltpu.VMEM((ch,), f32),
            pltpu.VMEM((ch,), f32),
            pltpu.VMEM((2 * ch,), f32),
            pltpu.VMEM((co,), f32),
            pltpu.VMEM((frames + 2, size, ch), bf16),
            pltpu.VMEM((frames * size, 2 * ch), f32),
            pltpu.VMEM((3, frames, 2, out_rows, cols, ch), bf16),
            pltpu.VMEM((2, 2 * frames, 2 * rows, 2 * cols, LANES), f32),
            pltpu.SemaphoreType.DMA((7,)),
            pltpu.SemaphoreType.DMA((9,)),
            pltpu.SemaphoreType.DMA((reach + 2,)),
            pltpu.SemaphoreType.DMA((reach + 2,)),
        ],
        compiler_params=pltpu.CompilerParams(collective_id=0, has_side_effects=True, vmem_limit_bytes=VMEM_BYTES - 2 * frames * 2 * rows * 2 * cols * (-(-co // LANES) * LANES) * 2),
    )(
        latent,
        w_in,
        b_in,
        gain_in,
        w_time,
        b_time,
        jnp.swapaxes(w_up, 2, 3),
        b_up,
    )


def solution(mesh):
    in_specs = (P(("clips", "tm"), "space", None, None), P(), P(), P(), P(), P(), P(), P())
    out_specs = P(("clips", "tm"), "space", None, None)
    body = functools.partial(shards, mesh.shape["tm"], mesh.shape["space"])
    return jax.shard_map(body, mesh=mesh, in_specs=in_specs, out_specs=out_specs, check_vma=False)
```

```python
import functools

import jax
import jax.numpy as jnp
from jax import lax
from jax.experimental import pallas as pl
from jax.experimental.pallas import tpu as pltpu
from jax.sharding import PartitionSpec as P

EPSILON = 1e-06
MESH = pl.DeviceIdType.MESH
LANES = 128
VMEM_BYTES = 67043328


def tap_groups(phase):
    return [(-1, (0,)), (0, (1, 2))] if phase == 0 else [(0, (0, 1)), (1, (2,))]


def kernel(
    sizes,
    lat_hbm,
    w_in_hbm,
    b_in_hbm,
    gain_hbm,
    w_time_hbm,
    b_time_hbm,
    w_up_hbm,
    b_up_hbm,
    out_v,
    lat_v,
    ext,
    taps,
    w_in_v,
    w_time_v,
    w_up_v,
    w_phase,
    b_in_v,
    gain_v,
    b_time_v,
    b_up_v,
    active,
    summed,
    shifted,
    wide,
    local_sem,
    w_in_sem,
    send_sem,
    recv_sem,
):
    tm_count, space_count, reach, frames, rows, cols, zc = sizes
    ch = w_time_v.shape[1]
    co = w_up_v.shape[2]
    halo = 1
    own_rows = rows
    out_rows = rows + 2
    tm = lax.axis_index("tm")
    space = lax.axis_index("space")
    direct = [(1, -1), (1, 1), (1, 0), (0, -1), (0, 1)]
    low, high = space > 0, space < space_count - 1
    later = tm < tm_count - 1

    def inside(d, o):
        t, s = tm + d, space + o
        return (t >= 0) & (t < tm_count) & (s >= 0) & (s < space_count)

    barrier = pltpu.get_barrier_semaphore()
    for d, o in direct:

        @pl.when(inside(-d, -o))
        def _():
            pl.semaphore_signal(
                barrier, inc=1, device_id={"tm": tm - d, "space": space - o}, device_id_type=MESH
            )

    lat_copy = pltpu.make_async_copy(lat_hbm, lat_v, local_sem.at[0])
    lat_copy.start()
    w_in_copies = [
        pltpu.make_async_copy(w_in_hbm.at[:, b, e], w_in_v.at[:, e, b], w_in_sem.at[3 * b + e])
        for b in range(3)
        for e in range(3)
    ]
    up_copy = pltpu.make_async_copy(w_up_hbm, w_up_v, local_sem.at[1])
    time_copy = pltpu.make_async_copy(w_time_hbm, w_time_v, local_sem.at[2])
    small_copies = [
        pltpu.make_async_copy(src, dst, local_sem.at[3 + i])
        for i, (src, dst) in enumerate(
            ((b_in_hbm, b_in_v), (gain_hbm, gain_v), (b_time_hbm, b_time_v), (b_up_hbm, b_up_v))
        )
    ]
    for copy in [up_copy] + w_in_copies + small_copies + [time_copy]:
        copy.start()

    for there, k in ((low, 0), (high, 2)):

        @pl.when(jnp.logical_not(there))
        def _():
            ext[reach, k] = jnp.zeros(ext.shape[2:], ext.dtype)

        @pl.when(jnp.logical_not(there) & (tm > 0))
        def _():
            ext[reach - 1, k] = jnp.zeros(ext.shape[2:], ext.dtype)

    for h in range(1, reach + 1):

        @pl.when(tm < h)
        def _():
            ext[reach - h] = jnp.zeros(ext.shape[1:], ext.dtype)

    w_in_v[:, :, 3] = jnp.zeros((3, 3) + w_in_v.shape[3:], w_in_v.dtype)

    lat_copy.wait()
    own = lat_v[...].astype(jnp.float32)
    pieces = [own[f, r] for f in range(frames) for r in range(rows)]
    pieces.append(jnp.zeros((cols, LANES - frames * rows * zc), jnp.float32))
    ext[reach, halo] = jnp.concatenate(pieces, axis=1).astype(ext.dtype)

    pl.semaphore_wait(barrier, sum(inside(d, o).astype(jnp.int32) for d, o in direct))

    def straight(d, o):
        slot = reach + 3 * d + o + 1
        return pltpu.make_async_remote_copy(
            src_ref=ext.at[reach, halo],
            dst_ref=ext.at[reach - d, halo - o],
            send_sem=send_sem.at[slot],
            recv_sem=recv_sem.at[slot],
            device_id={"tm": tm + d, "space": space + o},
            device_id_type=MESH,
        )

    def along_time(h):
        return pltpu.make_async_remote_copy(
            src_ref=ext.at[reach - h + 1],
            dst_ref=ext.at[reach - h],
            send_sem=send_sem.at[h - 1],
            recv_sem=recv_sem.at[h - 1],
            device_id={"tm": tm + 1},
            device_id_type=MESH,
        )

    for d, o in direct:

        @pl.when(inside(d, o))
        def _():
            straight(d, o).start()

    up_copy.wait()
    step = 16

    @pl.loop(0, co // step)
    def _(i):
        at = pl.multiple_of(i * step, step)
        w = [
            [w_up_v[b, e, pl.ds(at, step), :].astype(jnp.float32) for e in range(3)]
            for b in range(3)
        ]
        for q in range(2):
            for m, (_, es) in enumerate(tap_groups(q)):
                col = [sum(w[b][e] for e in es[1:]) + w[b][es[0]] if len(es) > 1 else w[b][es[0]] for b in range(3)]
                for p in range(2):
                    for n, (_, bs) in enumerate(tap_groups(p)):
                        both = col[bs[0]] + col[bs[1]] if len(bs) > 1 else col[bs[0]]
                        place = pl.ds((2 * n + m) * ch, ch)
                        w_phase[p, q, pl.ds(at, step), place] = both.astype(w_phase.dtype)

    def pass_on(h):
        @pl.when(later & (tm >= h - 1))
        def _():
            along_time(h).start()

    def landed(d, o):
        @pl.when(inside(-d, -o))
        def _():
            straight(d, o).wait_recv()

    def arrived(h):
        if h == 1:
            for o in (-1, 1, 0):
                landed(1, o)
        else:

            @pl.when(tm >= h)
            def _():
                along_time(h).wait_recv()

    for copy in w_in_copies + small_copies:
        copy.wait()

    lane = lax.broadcasted_iota(jnp.int32, (1, LANES), 1)
    col_id = lax.broadcasted_iota(jnp.int32, (out_rows * cols, 1), 0) % cols

    def gather_taps(first, last):
        for frame in range(first, last):
            j, f = divmod(frame, frames)
            base = f * rows * zc
            line = jnp.concatenate(
                [
                    ext[j, k].astype(jnp.float32)[:, base : base + rows * zc]
                    for k in range(3)
                ]
                + [jnp.zeros((cols, LANES - 3 * rows * zc), jnp.float32)],
                axis=1,
            )
            start = rows - 2
            turned = [
                pltpu.roll(line, (LANES - (start + q) * zc) % LANES, 1) if start + q else line
                for q in range(out_rows)
            ]
            mid = jnp.concatenate(turned, axis=0)
            mid = jnp.where(lane < 3 * zc, mid, 0.0)
            left = jnp.where(col_id == 0, 0.0, pltpu.roll(mid, 1, 0))
            right = jnp.where(col_id == cols - 1, 0.0, pltpu.roll(mid, out_rows * cols - 1, 0))
            pair = left + pltpu.roll(mid, 4 * zc, 1)
            taps[frame] = jnp.concatenate([pair, right[:, : 4 * zc]], axis=1).astype(taps.dtype)

    def entry(first, count):
        total = None
        for a in range(3):
            lhs = taps[pl.ds(first + a, count)].reshape(count * out_rows * cols, -1)
            term = jnp.dot(lhs, w_in_v[a].reshape(12 * zc, ch), preferred_element_type=jnp.float32)
            total = term if total is None else total + term
        hidden = total + b_in_v[...].reshape(1, ch)
        inverse = lax.rsqrt(jnp.mean(hidden * hidden, axis=1, keepdims=True) + EPSILON)
        v = hidden * inverse * gain_v[...].reshape(1, ch)
        return (v / (1.0 + jnp.exp(-v))).astype(active.dtype).reshape(count, out_rows * cols, ch)

    head = reach * frames - 4
    near = -(-2 // frames)
    for h in range(1, near + 1):
        arrived(h)
        if h < reach:
            pass_on(h + 1)
    landed(0, -1)
    landed(0, 1)
    gather_taps(head + 2, head + 4 + frames)
    active[pl.ds(2, frames)] = entry(head + 2, frames)
    time_copy.wait()
    size = out_rows * cols

    def times(first, count, tap):
        lhs = active[pl.ds(first, count)].reshape(count * size, ch)
        return jnp.dot(lhs, w_time_v[tap], preferred_element_type=jnp.float32)

    summed[...] = times(2, frames, 2) + b_time_v[...].reshape(1, 2 * ch)
    for tap in range(2):
        skip = 2 - tap
        if frames > skip:
            summed[skip * size :] = summed[skip * size :] + times(2, frames - skip, tap)

    for h in range(near + 1, reach + 1):
        arrived(h)
        if h < reach:
            pass_on(h + 1)
    gather_taps(head, head + 2)
    early = entry(head, 2)
    known = lax.broadcasted_iota(jnp.int32, (2, 1, 1), 0) + (tm * frames - 2) >= 0
    active[pl.ds(0, 2)] = jnp.where(known, early, jnp.zeros_like(early))
    for tap in range(2):
        n = min(2 - tap, frames)
        summed[: n * size] = summed[: n * size] + times(tap, n, tap)

    row_id = lax.broadcasted_iota(jnp.int32, (frames * size, 1), 0) % size // cols
    column = lax.broadcasted_iota(jnp.int32, (frames * size, 1), 0) % cols
    row_ok = ((row_id > 0) | (space > 0)) & ((row_id < out_rows - 1) | (space < space_count - 1))
    for half in range(2):
        part = summed[:, half * ch : (half + 1) * ch].astype(shifted.dtype).astype(jnp.float32)
        part = jnp.where(row_ok, part, 0.0)
        back = jnp.where(column == 0, 0.0, pltpu.roll(part, 1, 0))
        ahead = jnp.where(column == cols - 1, 0.0, pltpu.roll(part, frames * size - 1, 0))
        for i, moved in enumerate((back, part, ahead)):
            shifted[i, :, half] = moved.astype(shifted.dtype).reshape(frames, out_rows, cols, ch)

    for p in range(2):
        for q in range(2):
            lhs = jnp.concatenate(
                [
                    shifted[1 + dc, :, :, pl.ds(1 + dr, own_rows)].reshape(
                        2 * frames * own_rows * cols, ch
                    )
                    for dr, _ in tap_groups(p)
                    for dc, _ in tap_groups(q)
                ],
                axis=1,
            )
            y = lax.dot_general(
                lhs, w_phase[p, q], (((1,), (1,)), ((), ())), preferred_element_type=jnp.float32
            )
            y = y + b_up_v[...].reshape(1, co)
            y = y.reshape(2 * frames, own_rows, cols, co)
            for g in range(2 * frames):
                for r in range(own_rows):
                    part = y[g, r]
                    first = part[:, :LANES]
                    wide[0, g, 2 * r + p, pl.ds(q, cols, stride=2), :] = first
                    rest = jnp.concatenate(
                        [part[:, LANES:], jnp.zeros((cols, 2 * LANES - co), jnp.float32)], axis=1
                    )
                    wide[1, g, 2 * r + p, pl.ds(q, cols, stride=2), :] = rest
        for r in range(own_rows):
            row = 2 * r + p
            out_v[:, row, :, :LANES] = wide[0, :, row].astype(out_v.dtype)
            out_v[:, row, :, LANES:] = wide[1, :, row][:, :, : co - LANES].astype(out_v.dtype)

    for d, o in direct:

        @pl.when(inside(d, o))
        def _():
            straight(d, o).wait_send()

    for h in range(2, reach + 1):

        @pl.when(later & (tm >= h - 1))
        def _():
            along_time(h).wait_send()


def shards(tm_count, space_count, latent, w_in, b_in, gain_in, w_time, b_time, w_up, b_up):
    frames, rows, cols, zc = latent.shape
    ch, co = w_in.shape[-1], w_up.shape[-1]
    reach = -(-4 // frames)
    out_rows = rows + 2
    size = out_rows * cols
    bf16, f32 = jnp.bfloat16, jnp.float32
    any_spec = pl.BlockSpec(memory_space=pl.ANY)
    return pl.pallas_call(
        functools.partial(kernel, (tm_count, space_count, reach, frames, rows, cols, zc)),
        out_shape=pltpu.VMEM((2 * frames, 2 * rows, 2 * cols, co), bf16),
        in_specs=[any_spec] * 8,
        out_specs=pl.BlockSpec(memory_space=pltpu.VMEM),
        scratch_shapes=[
            pltpu.VMEM(latent.shape, bf16),
            pltpu.VMEM((reach + 1, 3, cols, LANES), bf16),
            pltpu.VMEM(((reach + 1) * frames, size, 12 * zc), bf16),
            pltpu.VMEM((3, 3, 4, zc, ch), bf16),
            pltpu.VMEM(w_time.shape, bf16),
            pltpu.VMEM((3, 3, co, ch), bf16),
            pltpu.VMEM((2, 2, co, 4 * ch), bf16),
            pltpu.VMEM((ch,), f32),
            pltpu.VMEM((ch,), f32),
            pltpu.VMEM((2 * ch,), f32),
            pltpu.VMEM((co,), f32),
            pltpu.VMEM((frames + 2, size, ch), bf16),
            pltpu.VMEM((frames * size, 2 * ch), f32),
            pltpu.VMEM((3, frames, 2, out_rows, cols, ch), bf16),
            pltpu.VMEM((2, 2 * frames, 2 * rows, 2 * cols, LANES), f32),
            pltpu.SemaphoreType.DMA((7,)),
            pltpu.SemaphoreType.DMA((9,)),
            pltpu.SemaphoreType.DMA((reach + 6,)),
            pltpu.SemaphoreType.DMA((reach + 6,)),
        ],
        compiler_params=pltpu.CompilerParams(collective_id=0, has_side_effects=True, vmem_limit_bytes=VMEM_BYTES - 2 * frames * 2 * rows * 2 * cols * (-(-co // LANES) * LANES) * 2),
    )(
        latent,
        w_in,
        b_in,
        gain_in,
        w_time,
        b_time,
        jnp.swapaxes(w_up, 2, 3),
        b_up,
    )


def solution(mesh):
    in_specs = (P(("clips", "tm"), "space", None, None), P(), P(), P(), P(), P(), P(), P())
    out_specs = P(("clips", "tm"), "space", None, None)
    body = functools.partial(shards, mesh.shape["tm"], mesh.shape["space"])
    return jax.shard_map(body, mesh=mesh, in_specs=in_specs, out_specs=out_specs, check_vma=False)
```

```python
import functools

import jax
import jax.numpy as jnp
from jax import lax
from jax.experimental import pallas as pl
from jax.experimental.pallas import tpu as pltpu
from jax.sharding import PartitionSpec as P

EPSILON = 1e-06
MESH = pl.DeviceIdType.MESH
LANES = 128
VMEM_BYTES = 67043328


def tap_groups(phase):
    return [(-1, (0,)), (0, (1, 2))] if phase == 0 else [(0, (0, 1)), (1, (2,))]


def kernel(
    sizes,
    lat_hbm,
    w_in_hbm,
    b_in_hbm,
    gain_hbm,
    w_time_hbm,
    b_time_hbm,
    w_up_hbm,
    b_up_hbm,
    out_v,
    lat_v,
    ext,
    taps,
    w_in_v,
    w_time_v,
    w_up_v,
    w_phase,
    w_flat,
    b_in_v,
    gain_v,
    b_time_v,
    b_up_v,
    active,
    summed,
    shifted,
    wide,
    local_sem,
    w_in_sem,
    send_sem,
    recv_sem,
):
    tm_count, space_count, reach, frames, rows, cols, zc = sizes
    ch = w_time_v.shape[1]
    co = w_up_v.shape[2]
    halo = 1
    own_rows = rows
    out_rows = rows + 2
    tm = lax.axis_index("tm")
    space = lax.axis_index("space")
    direct = [(1, -1), (1, 1), (1, 0), (0, -1), (0, 1)]
    low, high = space > 0, space < space_count - 1
    later = tm < tm_count - 1

    def inside(d, o):
        t, s = tm + d, space + o
        return (t >= 0) & (t < tm_count) & (s >= 0) & (s < space_count)

    barrier = pltpu.get_barrier_semaphore()
    for d, o in direct:

        @pl.when(inside(-d, -o))
        def _():
            pl.semaphore_signal(
                barrier, inc=1, device_id={"tm": tm - d, "space": space - o}, device_id_type=MESH
            )

    lat_copy = pltpu.make_async_copy(lat_hbm, lat_v, local_sem.at[0])
    lat_copy.start()
    w_in_copies = [
        pltpu.make_async_copy(w_in_hbm.at[:, b, e], w_in_v.at[:, e, b], w_in_sem.at[3 * b + e])
        for b in range(3)
        for e in range(3)
    ]
    up_copy = pltpu.make_async_copy(w_up_hbm, w_up_v, local_sem.at[1])
    time_copy = pltpu.make_async_copy(w_time_hbm, w_time_v, local_sem.at[2])
    small_copies = [
        pltpu.make_async_copy(src, dst, local_sem.at[3 + i])
        for i, (src, dst) in enumerate(
            ((b_in_hbm, b_in_v), (gain_hbm, gain_v), (b_time_hbm, b_time_v), (b_up_hbm, b_up_v))
        )
    ]
    for copy in [up_copy] + w_in_copies + small_copies + [time_copy]:
        copy.start()

    for there, k in ((low, 0), (high, 2)):

        @pl.when(jnp.logical_not(there))
        def _():
            ext[reach, k] = jnp.zeros(ext.shape[2:], ext.dtype)

        @pl.when(jnp.logical_not(there) & (tm > 0))
        def _():
            ext[reach - 1, k] = jnp.zeros(ext.shape[2:], ext.dtype)

    for h in range(1, reach + 1):

        @pl.when(tm < h)
        def _():
            ext[reach - h] = jnp.zeros(ext.shape[1:], ext.dtype)

    w_in_v[:, :, 3] = jnp.zeros((3, 3) + w_in_v.shape[3:], w_in_v.dtype)

    lat_copy.wait()
    own = lat_v[...].astype(jnp.float32)
    pieces = [own[f, r] for f in range(frames) for r in range(rows)]
    pieces.append(jnp.zeros((cols, LANES - frames * rows * zc), jnp.float32))
    ext[reach, halo] = jnp.concatenate(pieces, axis=1).astype(ext.dtype)

    pl.semaphore_wait(barrier, sum(inside(d, o).astype(jnp.int32) for d, o in direct))

    def straight(d, o):
        slot = reach + 3 * d + o + 1
        return pltpu.make_async_remote_copy(
            src_ref=ext.at[reach, halo],
            dst_ref=ext.at[reach - d, halo - o],
            send_sem=send_sem.at[slot],
            recv_sem=recv_sem.at[slot],
            device_id={"tm": tm + d, "space": space + o},
            device_id_type=MESH,
        )

    def along_time(h):
        return pltpu.make_async_remote_copy(
            src_ref=ext.at[reach - h + 1],
            dst_ref=ext.at[reach - h],
            send_sem=send_sem.at[h - 1],
            recv_sem=recv_sem.at[h - 1],
            device_id={"tm": tm + 1},
            device_id_type=MESH,
        )

    for d, o in direct:

        @pl.when(inside(d, o))
        def _():
            straight(d, o).start()

    up_copy.wait()
    step = 16

    @pl.loop(0, co // step)
    def _(i):
        at = pl.multiple_of(i * step, step)
        w = [
            [w_up_v[b, e, pl.ds(at, step), :].astype(jnp.float32) for e in range(3)]
            for b in range(3)
        ]
        for q in range(2):
            for m, (_, es) in enumerate(tap_groups(q)):
                col = [sum(w[b][e] for e in es[1:]) + w[b][es[0]] if len(es) > 1 else w[b][es[0]] for b in range(3)]
                for p in range(2):
                    for n, (_, bs) in enumerate(tap_groups(p)):
                        both = col[bs[0]] + col[bs[1]] if len(bs) > 1 else col[bs[0]]
                        place = pl.ds((2 * n + m) * ch, ch)
                        w_phase[p, q, pl.ds(at, step), place] = both.astype(w_phase.dtype)

    def pass_on(h):
        @pl.when(later & (tm >= h - 1))
        def _():
            along_time(h).start()

    for p in range(2):
        for q in range(2):
            w_flat[p, q] = w_phase[p, q].T

    def landed(d, o):
        @pl.when(inside(-d, -o))
        def _():
            straight(d, o).wait_recv()

    def arrived(h):
        if h == 1:
            for o in (-1, 1, 0):
                landed(1, o)
        else:

            @pl.when(tm >= h)
            def _():
                along_time(h).wait_recv()

    for copy in w_in_copies + small_copies:
        copy.wait()

    lane = lax.broadcasted_iota(jnp.int32, (1, LANES), 1)
    col_id = lax.broadcasted_iota(jnp.int32, (out_rows * cols, 1), 0) % cols

    def gather_taps(first, last):
        for frame in range(first, last):
            j, f = divmod(frame, frames)
            base = f * rows * zc
            line = jnp.concatenate(
                [
                    ext[j, k].astype(jnp.float32)[:, base : base + rows * zc]
                    for k in range(3)
                ]
                + [jnp.zeros((cols, LANES - 3 * rows * zc), jnp.float32)],
                axis=1,
            )
            start = rows - 2
            turned = [
                pltpu.roll(line, (LANES - (start + q) * zc) % LANES, 1) if start + q else line
                for q in range(out_rows)
            ]
            mid = jnp.concatenate(turned, axis=0)
            mid = jnp.where(lane < 3 * zc, mid, 0.0)
            left = jnp.where(col_id == 0, 0.0, pltpu.roll(mid, 1, 0))
            right = jnp.where(col_id == cols - 1, 0.0, pltpu.roll(mid, out_rows * cols - 1, 0))
            pair = left + pltpu.roll(mid, 4 * zc, 1)
            taps[frame] = jnp.concatenate([pair, right[:, : 4 * zc]], axis=1).astype(taps.dtype)

    def entry(first, count):
        total = None
        for a in range(3):
            lhs = taps[pl.ds(first + a, count)].reshape(count * out_rows * cols, -1)
            term = jnp.dot(lhs, w_in_v[a].reshape(12 * zc, ch), preferred_element_type=jnp.float32)
            total = term if total is None else total + term
        hidden = total + b_in_v[...].reshape(1, ch)
        inverse = lax.rsqrt(jnp.mean(hidden * hidden, axis=1, keepdims=True) + EPSILON)
        v = hidden * inverse * gain_v[...].reshape(1, ch)
        return (v / (1.0 + jnp.exp(-v))).astype(active.dtype).reshape(count, out_rows * cols, ch)

    head = reach * frames - 4
    near = -(-2 // frames)
    for h in range(1, near + 1):
        arrived(h)
        if h < reach:
            pass_on(h + 1)
    landed(0, -1)
    landed(0, 1)
    gather_taps(head + 2, head + 4 + frames)
    active[pl.ds(2, frames)] = entry(head + 2, frames)
    time_copy.wait()
    size = out_rows * cols

    def times(first, count, tap):
        lhs = active[pl.ds(first, count)].reshape(count * size, ch)
        return jnp.dot(lhs, w_time_v[tap], preferred_element_type=jnp.float32)

    summed[...] = times(2, frames, 2) + b_time_v[...].reshape(1, 2 * ch)
    for tap in range(2):
        skip = 2 - tap
        if frames > skip:
            summed[skip * size :] = summed[skip * size :] + times(2, frames - skip, tap)

    for h in range(near + 1, reach + 1):
        arrived(h)
        if h < reach:
            pass_on(h + 1)
    gather_taps(head, head + 2)
    early = entry(head, 2)
    known = lax.broadcasted_iota(jnp.int32, (2, 1, 1), 0) + (tm * frames - 2) >= 0
    active[pl.ds(0, 2)] = jnp.where(known, early, jnp.zeros_like(early))
    for tap in range(2):
        n = min(2 - tap, frames)
        summed[: n * size] = summed[: n * size] + times(tap, n, tap)

    row_id = lax.broadcasted_iota(jnp.int32, (frames * size, 1), 0) % size // cols
    column = lax.broadcasted_iota(jnp.int32, (frames * size, 1), 0) % cols
    row_ok = ((row_id > 0) | (space > 0)) & ((row_id < out_rows - 1) | (space < space_count - 1))
    for half in range(2):
        part = summed[:, half * ch : (half + 1) * ch].astype(shifted.dtype).astype(jnp.float32)
        part = jnp.where(row_ok, part, 0.0)
        back = jnp.where(column == 0, 0.0, pltpu.roll(part, 1, 0))
        ahead = jnp.where(column == cols - 1, 0.0, pltpu.roll(part, frames * size - 1, 0))
        for i, moved in enumerate((back, part, ahead)):
            shifted[i, :, half] = moved.astype(shifted.dtype).reshape(frames, out_rows, cols, ch)

    for p in range(2):
        for q in range(2):
            lhs = jnp.concatenate(
                [
                    shifted[1 + dc, :, :, pl.ds(1 + dr, own_rows)].reshape(
                        2 * frames * own_rows * cols, ch
                    )
                    for dr, _ in tap_groups(p)
                    for dc, _ in tap_groups(q)
                ],
                axis=1,
            )
            y = jnp.dot(lhs, w_flat[p, q], preferred_element_type=jnp.float32)
            y = y + b_up_v[...].reshape(1, co)
            y = y.reshape(2 * frames, own_rows, cols, co)
            for g in range(2 * frames):
                for r in range(own_rows):
                    part = y[g, r]
                    first = part[:, :LANES]
                    wide[0, g, 2 * r + p, pl.ds(q, cols, stride=2), :] = first
                    rest = jnp.concatenate(
                        [part[:, LANES:], jnp.zeros((cols, 2 * LANES - co), jnp.float32)], axis=1
                    )
                    wide[1, g, 2 * r + p, pl.ds(q, cols, stride=2), :] = rest
        for r in range(own_rows):
            row = 2 * r + p
            out_v[:, row, :, :LANES] = wide[0, :, row].astype(out_v.dtype)
            out_v[:, row, :, LANES:] = wide[1, :, row][:, :, : co - LANES].astype(out_v.dtype)

    for d, o in direct:

        @pl.when(inside(d, o))
        def _():
            straight(d, o).wait_send()

    for h in range(2, reach + 1):

        @pl.when(later & (tm >= h - 1))
        def _():
            along_time(h).wait_send()


def shards(tm_count, space_count, latent, w_in, b_in, gain_in, w_time, b_time, w_up, b_up):
    frames, rows, cols, zc = latent.shape
    ch, co = w_in.shape[-1], w_up.shape[-1]
    reach = -(-4 // frames)
    out_rows = rows + 2
    size = out_rows * cols
    bf16, f32 = jnp.bfloat16, jnp.float32
    any_spec = pl.BlockSpec(memory_space=pl.ANY)
    return pl.pallas_call(
        functools.partial(kernel, (tm_count, space_count, reach, frames, rows, cols, zc)),
        out_shape=pltpu.VMEM((2 * frames, 2 * rows, 2 * cols, co), bf16),
        in_specs=[any_spec] * 8,
        out_specs=pl.BlockSpec(memory_space=pltpu.VMEM),
        scratch_shapes=[
            pltpu.VMEM(latent.shape, bf16),
            pltpu.VMEM((reach + 1, 3, cols, LANES), bf16),
            pltpu.VMEM(((reach + 1) * frames, size, 12 * zc), bf16),
            pltpu.VMEM((3, 3, 4, zc, ch), bf16),
            pltpu.VMEM(w_time.shape, bf16),
            pltpu.VMEM((3, 3, co, ch), bf16),
            pltpu.VMEM((2, 2, co, 4 * ch), bf16),
            pltpu.VMEM((2, 2, 4 * ch, co), bf16),
            pltpu.VMEM((ch,), f32),
            pltpu.VMEM((ch,), f32),
            pltpu.VMEM((2 * ch,), f32),
            pltpu.VMEM((co,), f32),
            pltpu.VMEM((frames + 2, size, ch), bf16),
            pltpu.VMEM((frames * size, 2 * ch), f32),
            pltpu.VMEM((3, frames, 2, out_rows, cols, ch), bf16),
            pltpu.VMEM((2, 2 * frames, 2 * rows, 2 * cols, LANES), f32),
            pltpu.SemaphoreType.DMA((7,)),
            pltpu.SemaphoreType.DMA((9,)),
            pltpu.SemaphoreType.DMA((reach + 6,)),
            pltpu.SemaphoreType.DMA((reach + 6,)),
        ],
        compiler_params=pltpu.CompilerParams(collective_id=0, has_side_effects=True, vmem_limit_bytes=VMEM_BYTES - 2 * frames * 2 * rows * 2 * cols * (-(-co // LANES) * LANES) * 2),
    )(
        latent,
        w_in,
        b_in,
        gain_in,
        w_time,
        b_time,
        jnp.swapaxes(w_up, 2, 3),
        b_up,
    )


def solution(mesh):
    in_specs = (P(("clips", "tm"), "space", None, None), P(), P(), P(), P(), P(), P(), P())
    out_specs = P(("clips", "tm"), "space", None, None)
    body = functools.partial(shards, mesh.shape["tm"], mesh.shape["space"])
    return jax.shard_map(body, mesh=mesh, in_specs=in_specs, out_specs=out_specs, check_vma=False)
```
